32 devices in a mesh: frame: 4 (over x, core), within: 8 (over z, y).
Axes of the slice: x: 2, y: 2, z: 4, core: 2. Of those that a mesh axis runs over, the one named last changes fastest.
Arguments:
- queries: bfloat16 [4, 576, 1024], P('frame', 'within'), may hold values from -6 to 6
- keys_in: bfloat16 [4, 576, 1024], P('frame', 'within'), may hold values from -6 to 6
- values_in: bfloat16 [4, 576, 1024], P('frame', 'within'), may hold values from -6 to 6
- grad_out: bfloat16 [4, 576, 1024], P('frame', 'within'), may hold values from -6 to 6
- partners: int32 [4, 2], replicated, may hold values from 0 to 3
- registers: int32 [4], replicated, may hold values from 1 to 144
Outputs:
- grad_queries: bfloat16 [4, 576, 1024], P('frame', 'within')
- grad_keys: bfloat16 [4, 576, 1024], P('frame', 'within')
- grad_values: bfloat16 [4, 576, 1024], P('frame', 'within')
The draws below stay inside these ranges and needn't reach their ends.
Inputs may be any that keep to these rules, and one draw needn't show every extreme that they name: `partners`: A row may list a group more than once, and may list its own group.
All inputs are finite; a program needn't handle non-finite values.
Results may differ from the reference program's by a relative error of at most 0.012.
Values may be sent and summed in bfloat16 or wider, within the bound.
A program may use at most 128 MiB of HBM per device.

```python
import math
import jax
import jax.numpy as jnp
import numpy as np
from jax import lax

HEADS = 16
DH = 64
D = 1024
PART = 2
G = 4
S = 576


def draw_queries(key, part):
    base = jnp.clip(jax.random.normal(jax.random.fold_in(key, 1), (G, S, D), jnp.float32), -6.0, 6.0)
    return base.astype(jnp.bfloat16)


def draw_keys_in(key, part):
    base = jnp.clip(jax.random.normal(jax.random.fold_in(key, 2), (G, S, D), jnp.float32), -6.0, 6.0)
    return base.astype(jnp.bfloat16)


def set_ends(entries, own_key, least, top_value):
    shape = entries.shape
    place = [jax.random.randint(jax.random.fold_in(own_key, axis), (), 0, shape[axis]) for axis in range(len(shape))]
    entries = entries.at[tuple(place)].set(least)
    longest = shape.index(max(shape))
    place[longest] = (place[longest] + 1) % shape[longest]
    return entries.at[tuple(place)].set(top_value)


def block_scale(own_key, shape, pieces, low, high):
    def one(position, shards_of):
        steps = jax.random.uniform(jax.random.fold_in(jax.random.fold_in(own_key, 6), position), (shards_of,), jnp.float32, low / len(pieces), high / len(pieces))
        return jnp.repeat(jnp.exp(steps), shape[position] // shards_of).reshape((-1,) + (1,) * (len(shape) - position - 1))

    factor_of = one(*pieces[0])
    for cut in pieces[1:]:
        factor_of = factor_of * one(*cut)
    return factor_of


def cumulative_ranks(amount, slope):
    portions = [(1 << 20) // math.isqrt(rank ** slope) + 1 for rank in range(1, amount + 1)]
    scale = 1 + sum(portions) // (1 << 30)
    return np.cumsum(np.array([max(1, weight // scale) for weight in portions]))


def ranked_ids(stream_key, shape, count, skew):
    table = cumulative_ranks(count, skew)
    pick = jax.random.randint(jax.random.fold_in(stream_key, 1), shape, 0, int(table[count - 1]))
    rank = jnp.searchsorted(jnp.asarray(table, jnp.int32), pick, side="right")
    return jax.random.permutation(jax.random.fold_in(stream_key, 2), count)[rank].astype(jnp.int32)


def normal_values(stream_key, dims, spread, bound, pieces=(), held_as=jnp.bfloat16):
    gain = block_scale(stream_key, dims, pieces, -0.22, 0.18) if pieces else 1.0
    drawn = jax.random.normal(stream_key, dims, jnp.float32) * spread * gain
    return jnp.minimum(jnp.maximum(drawn, -bound), bound).astype(held_as)


def setup_inputs(seed: int = 0) -> dict:
    arg_keys = jax.random.split(jax.random.key(seed), 7)
    queries = draw_queries(jax.random.fold_in(arg_keys[6], 71), 0)
    keys_in = draw_keys_in(jax.random.fold_in(arg_keys[6], 71), 0)
    values_in = normal_values(arg_keys[2], (G, S, D), 1.0, 6.0, ((0, 4), (1, 8)))
    grad_out = normal_values(arg_keys[3], (G, S, D), 1.0, 6.0, ((0, 4), (1, 8)))
    partners = set_ends(ranked_ids(arg_keys[4], (G, PART), G, 2), jax.random.fold_in(arg_keys[4], 3), 0, G - 1).astype(jnp.int32)
    registers = set_ends(jax.random.randint(arg_keys[5], (G,), 1, S // 4 + 1), jax.random.fold_in(arg_keys[5], 1), 1, (S // 4 + 1) - 1).astype(jnp.int32)
    return dict(queries=queries, keys_in=keys_in, values_in=values_in, grad_out=grad_out, partners=partners, registers=registers)


def reference(queries, keys_in, values_in, grad_out, partners, registers):
    groups, seq, width = queries.shape
    scale = DH ** -0.5
    positions = jnp.arange(seq).astype(jnp.int32)

    def head_split(block):
        return block.reshape(block.shape[0], HEADS, DH).transpose(1, 0, 2)

    def one_head(operands):
        qh, kh, vh, dh, visible = operands
        raw = jnp.dot(qh, kh.T, preferred_element_type=jnp.float32) * scale
        raw = jnp.where(visible[None, :], raw, -1e30)
        top = jnp.max(raw, axis=1, keepdims=True)
        expo = jnp.exp(raw - top)
        prob = expo / jnp.sum(expo, axis=1, keepdims=True)
        dprod = jnp.dot(dh, vh.T, preferred_element_type=jnp.float32)
        delta = jnp.sum(prob * dprod, axis=1, keepdims=True)
        dscore = prob * (dprod - delta)
        prob_low = prob.astype(jnp.bfloat16)
        dscore_low = dscore.astype(jnp.bfloat16)
        dq = jnp.dot(dscore_low, kh, preferred_element_type=jnp.float32) * scale
        dk = jnp.dot(dscore_low.T, qh, preferred_element_type=jnp.float32) * scale
        dv = jnp.dot(prob_low.T, dh, preferred_element_type=jnp.float32)
        return dq, dk, dv

    def one_group(carry, index):
        dk_all, dv_all = carry
        listed = jnp.concatenate([index[None].astype(jnp.int32), partners[index].astype(jnp.int32)])
        keys_list = keys_in[listed].reshape(-1, width)
        values_list = values_in[listed].reshape(-1, width)
        hidden_regs = positions[None, :] >= registers[partners[index]][:, None]
        visible = jnp.concatenate([jnp.ones((seq,), dtype=bool), hidden_regs.reshape(-1)])
        visible_all = jnp.broadcast_to(visible[None, :], (HEADS, visible.shape[0]))
        dq, dk, dv = lax.map(one_head, (head_split(queries[index]), head_split(keys_list),
                                        head_split(values_list), head_split(grad_out[index]), visible_all))
        dq = dq.transpose(1, 0, 2).reshape(seq, width)
        dk = dk.transpose(1, 0, 2).reshape(PART + 1, seq, width)
        dv = dv.transpose(1, 0, 2).reshape(PART + 1, seq, width)
        dk_all = dk_all.at[listed].add(dk)
        dv_all = dv_all.at[listed].add(dv)
        return (dk_all, dv_all), dq.astype(jnp.bfloat16)

    start = (jnp.zeros((groups, seq, width), jnp.float32), jnp.zeros((groups, seq, width), jnp.float32))
    (dk_all, dv_all), grad_queries = lax.scan(one_group, start, jnp.arange(groups).astype(jnp.int32))
    return grad_queries, dk_all.astype(jnp.bfloat16), dv_all.astype(jnp.bfloat16)
```

```python
import functools
import math

import jax
import jax.numpy as jnp
import numpy as np
from jax import lax
from jax.experimental import pallas as pl
from jax.experimental.pallas import tpu as pltpu
from jax.sharding import PartitionSpec as P

DH = 64
PAIR = 2 * DH
SPLITS = 3
HIDDEN = -1e30
BF = jnp.bfloat16
F32 = jnp.float32
MESH = pl.DeviceIdType.MESH


def pieces_of(value):
    left, out = float(value), []
    for _ in range(SPLITS):
        part = float(np.asarray(left, dtype=jnp.bfloat16))
        out.append(part)
        left = left - part if abs(value) < 1e20 else 0.0
    return out


def rdot(a, b):
    return lax.dot_general(a, b, (((1,), (1,)), ((), ())), preferred_element_type=F32)


def dot(a, b):
    return jnp.dot(a, b, preferred_element_type=F32)


def kernel(F, W, R, QB, part_ref, reg_ref, q_ref, k_ref, v_ref, d_ref, dq_out, dk_out, dv_out,
           kv_send, qd_send, kv_in, qd_in, kaug, vz, kt, qaug, xraw, qz, doz, sbuf, dpbuf, acc, dqs,
           red_send, red_in, fin_send, fin_in, dq_send, dq_in,
           kv_ss, fw_ss, kv_rs, qd_ss, qd_rs, red_ss, red_rs, fin_ss, fin_rs, dq_ss, dq_rs):
    fs = F // R
    half_f = F // 2
    rows = q_ref.shape[1]
    width = q_ref.shape[2]
    seq = rows * W
    n_slots = part_ref.shape[1]
    scale = DH ** -0.5
    half = dq_send.shape[2]
    nq = R * seq
    f = lax.axis_index("frame")
    w = lax.axis_index("within")
    c = lax.rem(f, fs)
    a0 = lax.div(f, fs)
    sib = f + 1 - 2 * lax.rem(f, 2)
    head = w * R + a0

    barrier = pltpu.get_barrier_semaphore()

    def greet(t, carry):
        ff = lax.rem(f + 2 * lax.div(t, W), F)
        ww = lax.rem(w + lax.rem(t, W), W)
        pl.semaphore_signal(barrier, inc=1, device_id=(ff, ww), device_id_type=MESH)
        return carry

    lax.fori_loop(1, half_f * W, greet, 0)
    for dc in range(1, fs, 2):
        pl.semaphore_signal(barrier, inc=1, device_id=(a0 * fs + lax.rem(c + dc, fs), w), device_id_type=MESH)

    for j in range(width // PAIR):
        cols = slice(j * PAIR, (j + 1) * PAIR)
        for first, second, out in ((k_ref, v_ref, kv_send), (q_ref, d_ref, qd_send)):
            one = first[0, :, cols]
            two = second[0, :, cols]
            out[2 * j] = jnp.concatenate([one[:, :DH], two[:, :DH]], axis=1)
            out[2 * j + 1] = jnp.concatenate([one[:, DH:], two[:, DH:]], axis=1)
    kv_in[f, w] = kv_send[head]
    qd_in[a0, w] = qd_send[head]

    pl.semaphore_wait(barrier, half_f * W - 1 + fs // 2)

    def kv_copy(t):
        ff = lax.rem(f + 2 * lax.div(t, W), F)
        ww = lax.rem(w + lax.rem(t, W), W)
        return pltpu.make_async_remote_copy(
            src_ref=kv_send.at[ww * R + lax.div(ff, fs)], dst_ref=kv_in.at[f, w],
            send_sem=kv_ss.at[t], recv_sem=kv_rs.at[f * W + w],
            device_id=(ff, ww), device_id_type=MESH)

    def forward(t):
        ff = lax.rem(f + F - 2 * lax.div(t, W), F)
        ww = lax.rem(w + W - lax.rem(t, W), W)
        return pltpu.make_async_remote_copy(
            src_ref=kv_in.at[ff, ww], dst_ref=kv_in.at[ff, ww],
            send_sem=fw_ss.at[t], recv_sem=kv_rs.at[ff * W + ww],
            device_id=(sib, w), device_id_type=MESH)

    def from_sibling(t):
        ff = lax.rem(sib + F - 2 * lax.div(t, W), F)
        ww = lax.rem(w + W - lax.rem(t, W), W)
        return pltpu.make_async_remote_copy(
            src_ref=kv_in.at[ff, ww], dst_ref=kv_in.at[ff, ww],
            send_sem=fw_ss.at[t], recv_sem=kv_rs.at[ff * W + ww],
            device_id=(sib, w), device_id_type=MESH)

    def peer(t):
        return lax.rem(a0 + lax.div(t, W), R), lax.rem(w + lax.rem(t, W), W)

    def source(t):
        return lax.rem(a0 + R - lax.div(t, W), R), lax.rem(w + W - lax.rem(t, W), W)

    def qd_copy(t):
        aa, ww = peer(t)
        return pltpu.make_async_remote_copy(
            src_ref=qd_send.at[ww * R + aa], dst_ref=qd_in.at[a0, w],
            send_sem=qd_ss.at[t], recv_sem=qd_rs.at[a0 * W + w],
            device_id=(aa * fs + c, ww), device_id_type=MESH)

    def qd_arrival(t):
        aa, ww = source(t)
        return pltpu.make_async_remote_copy(
            src_ref=qd_in.at[aa, ww], dst_ref=qd_in.at[aa, ww],
            send_sem=qd_ss.at[t], recv_sem=qd_rs.at[aa * W + ww],
            device_id=(aa * fs + c, ww), device_id_type=MESH)

    def each(lo, hi, do):
        def step(t, carry):
            do(t)
            return carry
        lax.fori_loop(lo, hi, step, 0)

    forward(0).start()
    each(1, half_f * W, lambda t: kv_copy(t).start())
    each(1, R * W, lambda t: qd_copy(t).start())

    acc[...] = jnp.zeros_like(acc)

    def relay(t):
        move = forward(t)
        move.wait_recv()
        move.start()

    each(1, half_f * W, relay)
    each(0, half_f * W, lambda t: from_sibling(t).wait_recv())

    lane = lax.broadcasted_iota(jnp.int32, (seq, PAIR), 1)
    row = lax.broadcasted_iota(jnp.int32, (seq, PAIR), 0)
    lane1 = lax.broadcasted_iota(jnp.int32, (1, PAIR), 1)
    table = [pieces_of(HIDDEN)] + [pieces_of(math.log(n)) for n in range(1, n_slots + 2)]

    def prepare_keys(p):
        both = kv_in[p].astype(F32).reshape(seq, PAIR)
        seen = jnp.zeros((1, PAIR), F32)
        unseen = jnp.zeros((1, PAIR), F32)
        for gi in range(R):
            g = c + fs * gi
            own = jnp.where(p == g, 1, 0)
            count = own
            for slot in range(n_slots):
                count = count + jnp.where(part_ref[g, slot] == p, 1, 0)
            for e in range(SPLITS):
                here = lane1 == DH + SPLITS * gi + e
                for n in range(n_slots + 2):
                    if n < 2:
                        unseen = jnp.where(here & (own == n), table[n][e], unseen)
                    seen = jnp.where(here & (count == n), table[n][e], seen)
        extra = jnp.where(row >= reg_ref[p], seen, unseen)
        kaug[p] = jnp.where(lane < DH, both, extra).astype(BF)
        vz[p] = jnp.where(lane >= DH, both, 0.0).astype(BF)
        kt[p] = (both * scale).T[:DH].astype(BF)

    each(0, F, prepare_keys)
    each(1, R * W, lambda t: qd_arrival(t).wait_recv())

    for gi in range(R):
        both = qd_in[gi].astype(F32).reshape(seq, PAIR)
        at = slice(gi * seq, (gi + 1) * seq)
        mark = jnp.where((lane >= DH + SPLITS * gi) & (lane < DH + SPLITS * (gi + 1)), 1.0, 0.0)
        scaled = both * scale
        qaug[at] = jnp.where(lane < DH, scaled, mark).astype(BF)
        xraw[at] = both.astype(BF)
        qz[at] = jnp.where(lane < DH, scaled, 0.0).astype(BF)
        doz[at] = jnp.where(lane >= DH, both, 0.0).astype(BF)

    def block(i):
        at = pl.ds(pl.multiple_of(i * QB, QB), QB)

        def scores(p, top):
            raw = rdot(kaug[p], qaug[at])
            sbuf[p] = raw
            return jnp.maximum(top, jnp.max(raw, axis=0, keepdims=True))

        top = lax.fori_loop(0, F, scores, jnp.full((1, QB), -3e38, F32))

        def sums(p, state):
            total, dsum = state
            expo = jnp.exp(sbuf[p] - top)
            dprod = rdot(vz[p], xraw[at])
            sbuf[p] = expo
            dpbuf[p] = dprod
            return (total + jnp.sum(expo, axis=0, keepdims=True),
                    dsum + jnp.sum(expo * dprod, axis=0, keepdims=True))

        blank = jnp.zeros((1, QB), F32)
        total, dsum = lax.fori_loop(0, F, sums, (blank, blank))
        inv = 1.0 / total
        delta = dsum * inv

        def grads(p, dq):
            prob = sbuf[p] * inv
            dscore = (prob * (dpbuf[p] - delta)).astype(BF)
            acc[p] += dot(dscore, qz[at]) + dot(prob.astype(BF), doz[at])
            return dq + dot(kt[p], dscore)

        dq = lax.fori_loop(0, F, grads, jnp.zeros((DH, QB), F32))
        dqs[at] = jnp.concatenate([dq, jnp.zeros((DH, QB), F32)], axis=0).T

    each(0, nq // QB, block)

    def red_copy(dc, gi):
        cp = lax.rem(c + dc, fs)
        return pltpu.make_async_remote_copy(
            src_ref=red_send.at[dc - 1, gi], dst_ref=red_in.at[dc - 1, gi],
            send_sem=red_ss.at[(dc - 1) * R + gi], recv_sem=red_rs.at[(dc - 1) * R + gi],
            device_id=(a0 * fs + cp, w), device_id_type=MESH)

    for dc in range(1, fs):
        cp = lax.rem(c + dc, fs)
        for gi in range(R):
            red_send[dc - 1, gi] = acc[cp + fs * gi].reshape(W, rows, PAIR).astype(BF)
            red_copy(dc, gi).start()

    def dq_copy(t):
        aa, ww = peer(t)
        return pltpu.make_async_remote_copy(
            src_ref=dq_send.at[aa, ww], dst_ref=dq_in.at[head],
            send_sem=dq_ss.at[t], recv_sem=dq_rs.at[head],
            device_id=(aa * fs + c, ww), device_id_type=MESH)

    def dq_arrival(t):
        aa, ww = source(t)
        return pltpu.make_async_remote_copy(
            src_ref=dq_in.at[ww * R + aa], dst_ref=dq_in.at[ww * R + aa],
            send_sem=dq_ss.at[t], recv_sem=dq_rs.at[ww * R + aa],
            device_id=(aa * fs + c, ww), device_id_type=MESH)

    def fin_copy(t):
        aa, ww = peer(t)
        return pltpu.make_async_remote_copy(
            src_ref=fin_send.at[aa, ww], dst_ref=fin_in.at[head],
            send_sem=fin_ss.at[t], recv_sem=fin_rs.at[head],
            device_id=(aa * fs + c, ww), device_id_type=MESH)

    def fin_arrival(t):
        aa, ww = source(t)
        return pltpu.make_async_remote_copy(
            src_ref=fin_in.at[ww * R + aa], dst_ref=fin_in.at[ww * R + aa],
            send_sem=fin_ss.at[t], recv_sem=fin_rs.at[ww * R + aa],
            device_id=(aa * fs + c, ww), device_id_type=MESH)

    for gi in range(R):
        for ww in range(W):
            base = gi * seq + ww * rows
            dq_send[gi, ww] = jnp.concatenate(
                [dqs[base:base + half, :DH], dqs[base + rows - half:base + rows, :DH]], axis=1).astype(BF)
    dq_in[head] = dq_send[a0, w]
    each(1, R * W, lambda t: dq_copy(t).start())

    for gi in range(R):
        whole = acc[c + fs * gi].reshape(W, rows, PAIR)
        for dc in range(1, fs):
            red_copy(dc, gi).wait_recv()
            whole = whole + red_in[dc - 1, gi].astype(F32)
        fin_send[gi] = whole.astype(BF)
    fin_in[head] = fin_send[a0, w]
    each(1, R * W, lambda t: fin_copy(t).start())

    each(1, R * W, lambda t: dq_arrival(t).wait_recv())
    for j in range(width // PAIR):
        cols = slice(j * PAIR, (j + 1) * PAIR)
        sides = []
        for h in (2 * j, 2 * j + 1):
            got = dq_in[h].astype(F32)
            sides.append(jnp.concatenate([got[:, :DH], got[2 * half - rows:, DH:]], axis=0))
        dq_out[0, :, cols] = jnp.concatenate(sides, axis=1).astype(BF)

    each(1, R * W, lambda t: fin_arrival(t).wait_recv())
    for j in range(width // PAIR):
        cols = slice(j * PAIR, (j + 1) * PAIR)
        one, two = fin_in[2 * j], fin_in[2 * j + 1]
        dk_out[0, :, cols] = jnp.concatenate([one[:, :DH], two[:, :DH]], axis=1)
        dv_out[0, :, cols] = jnp.concatenate([one[:, DH:], two[:, DH:]], axis=1)

    each(1, half_f * W, lambda t: kv_copy(t).wait_send())
    each(0, half_f * W, lambda t: forward(t).wait_send())
    each(1, R * W, lambda t: qd_copy(t).wait_send())
    each(1, R * W, lambda t: dq_copy(t).wait_send())
    each(1, R * W, lambda t: fin_copy(t).wait_send())
    for dc in range(1, fs):
        for gi in range(R):
            red_copy(dc, gi).wait_send()


def local(F, W, queries, keys_in, values_in, grad_out, partners, registers):
    _, rows, width = queries.shape
    heads = width // DH
    R = heads // W
    fs = F // R
    seq = rows * W
    nq = R * seq
    half = ((rows + 1) // 2 + 7) // 8 * 8
    QB = next(b for b in (384, 256, 128) if nq % b == 0 and F * seq * b * 8 <= 20 * 2 ** 20)
    vm = lambda *shape: pltpu.VMEM(shape, BF)
    vf = lambda *shape: pltpu.VMEM(shape, F32)
    dma = lambda n: pltpu.SemaphoreType.DMA((n,))
    out = jax.ShapeDtypeStruct((1, rows, width), BF)
    return pl.pallas_call(
        functools.partial(kernel, F, W, R, QB),
        out_shape=(out, out, out),
        in_specs=[pl.BlockSpec(memory_space=pltpu.SMEM)] * 2 + [pl.BlockSpec(memory_space=pltpu.VMEM)] * 4,
        out_specs=(pl.BlockSpec(memory_space=pltpu.VMEM),) * 3,
        scratch_shapes=[
            vm(heads, rows, PAIR), vm(heads, rows, PAIR),
            vm(F, W, rows, PAIR), vm(R, W, rows, PAIR),
            vm(F, seq, PAIR), vm(F, seq, PAIR), vm(F, DH, seq),
            vm(nq, PAIR), vm(nq, PAIR), vm(nq, PAIR), vm(nq, PAIR),
            vf(F, seq, QB), vf(F, seq, QB), vf(F, seq, PAIR), vf(nq, PAIR),
            vm(fs - 1, R, W, rows, PAIR), vm(fs - 1, R, W, rows, PAIR),
            vm(R, W, rows, PAIR), vm(heads, rows, PAIR),
            vm(R, W, half, PAIR), vm(heads, half, PAIR),
            dma(F // 2 * W), dma(F // 2 * W), dma(F * W), dma(R * W), dma(R * W),
            dma((fs - 1) * R), dma((fs - 1) * R), dma(R * W), dma(heads), dma(R * W), dma(heads),
        ],
        compiler_params=pltpu.CompilerParams(
            collective_id=0, has_side_effects=True, vmem_limit_bytes=60 * 2 ** 20),
    )(partners, registers, queries, keys_in, values_in, grad_out)


def solution(mesh):
    spec = P("frame", "within", None)
    return jax.shard_map(
        functools.partial(local, mesh.shape["frame"], mesh.shape["within"]),
        mesh=mesh,
        in_specs=(spec, spec, spec, spec, P(), P()),
        out_specs=(spec, spec, spec),
        check_vma=False,
    )
```

```python
import functools
import math

import jax
import jax.numpy as jnp
import numpy as np
from jax import lax
from jax.experimental import pallas as pl
from jax.experimental.pallas import tpu as pltpu
from jax.sharding import PartitionSpec as P

DH = 64
PAIR = 2 * DH
SPLITS = 3
UNIT = 640
HIDDEN = -1e30
BF = jnp.bfloat16
F32 = jnp.float32
MESH = pl.DeviceIdType.MESH


def pieces_of(value):
    left, out = float(value), []
    for _ in range(SPLITS):
        part = float(np.asarray(left, dtype=jnp.bfloat16))
        out.append(part)
        left = left - part if abs(value) < 1e20 else 0.0
    return out


def rdot(a, b):
    return lax.dot_general(a, b, (((1,), (1,)), ((), ())), preferred_element_type=F32)


def dot(a, b):
    return jnp.dot(a, b, preferred_element_type=F32)


def each(lo, hi, do):
    def step(t, carry):
        do(t)
        return carry
    lax.fori_loop(lo, hi, step, 0)


def kernel(F, W, R, QC, inline, part_ref, reg_ref, q_ref, k_ref, v_ref, d_ref, dq_out, dk_out, dv_out,
           kv_send, qd_send, kv_in, qd_in, kaug, vz, kt, qaug, xraw, qdz, sbuf, dpbuf, acc, dqacc, dqs,
           tops, top_ref, total_ref, dsum_ref,
           red_send, red_in, fin_send, fin_in, dq_send, dq_in,
           kv_ss, fw_ss, kv_rs, qd_ss, qd_rs, red_ss, red_rs, fin_ss, fin_rs, dq_ss, dq_rs):
    fs = F // R
    hf = F // 2
    rows = q_ref.shape[1]
    width = q_ref.shape[2]
    seq = rows * W
    n_slots = part_ref.shape[0]
    scale = DH ** -0.5
    half = dq_send.shape[2]
    nq = R * seq
    n_chunks = nq // QC
    n_units, per = acc.shape[0], acc.shape[1]
    unit = per * F * rows
    f = lax.axis_index("frame")
    w = lax.axis_index("within")
    c = lax.rem(f, fs)
    a0 = lax.div(f, fs)
    sib = f + 1 - 2 * lax.rem(f, 2)
    head = w * R + a0

    barrier = pltpu.get_barrier_semaphore()

    def ahead(dw):
        return lax.rem(w + dw, W)

    def behind(dw):
        return lax.rem(w + W - dw, W)

    def greet(t):
        pl.semaphore_signal(barrier, inc=1, device_id=(lax.rem(f + 2 * lax.rem(t, hf), F), ahead(lax.div(t, hf))),
                            device_id_type=MESH)

    each(1, hf * W, greet)
    for dc in range(1, fs, 2):
        pl.semaphore_signal(barrier, inc=1, device_id=(a0 * fs + lax.rem(c + dc, fs), w), device_id_type=MESH)

    for first, second, out in ((q_ref, d_ref, qd_send), (k_ref, v_ref, kv_send)):
        for j in range(width // PAIR):
            cols = slice(j * PAIR, (j + 1) * PAIR)
            one = first[0, :, cols]
            two = second[0, :, cols]
            out[2 * j] = jnp.concatenate([one[:, :DH], two[:, :DH]], axis=1)
            out[2 * j + 1] = jnp.concatenate([one[:, DH:], two[:, DH:]], axis=1)
    kv_in[f, w] = kv_send[head]
    qd_in[a0, w] = qd_send[head]

    pl.semaphore_wait(barrier, hf * W - 1 + fs // 2)

    def kv_copy(t):
        ff = lax.rem(f + 2 * lax.rem(t, hf), F)
        ww = ahead(lax.div(t, hf))
        return pltpu.make_async_remote_copy(
            src_ref=kv_send.at[ww * R + lax.div(ff, fs)], dst_ref=kv_in.at[f, w],
            send_sem=kv_ss.at[t], recv_sem=kv_rs.at[f * W + w],
            device_id=(ff, ww), device_id_type=MESH)

    def pass_on(origin, t):
        ff = lax.rem(origin + F - 2 * lax.rem(t, hf), F)
        ww = behind(lax.div(t, hf))
        return pltpu.make_async_remote_copy(
            src_ref=kv_in.at[ff, ww], dst_ref=kv_in.at[ff, ww],
            send_sem=fw_ss.at[t], recv_sem=kv_rs.at[ff * W + ww],
            device_id=(sib, w), device_id_type=MESH)

    def qd_copy(t):
        aa, ww = lax.rem(a0 + lax.rem(t, R), R), ahead(lax.div(t, R))
        return pltpu.make_async_remote_copy(
            src_ref=qd_send.at[ww * R + aa], dst_ref=qd_in.at[a0, w],
            send_sem=qd_ss.at[t], recv_sem=qd_rs.at[a0 * W + w],
            device_id=(aa * fs + c, ww), device_id_type=MESH)

    def arrival(t, buffer, send, recv, index, source):
        return pltpu.make_async_remote_copy(
            src_ref=buffer.at[index], dst_ref=buffer.at[index], send_sem=send.at[t], recv_sem=recv,
            device_id=source, device_id_type=MESH)

    def qd_arrival(t):
        aa, ww = lax.rem(a0 + R - lax.rem(t, R), R), behind(lax.div(t, R))
        return arrival(t, qd_in, qd_ss, qd_rs.at[aa * W + ww], (aa, ww), (aa * fs + c, ww))

    def head_arrival(t, buffer, send, recv):
        aa, ww = lax.rem(a0 + R - lax.rem(t, R), R), ahead(lax.div(t, R))
        return arrival(t, buffer, send, recv.at[ww * R + aa], (ww * R + aa,), (aa * fs + c, ww))

    each(1, R * W, lambda t: qd_copy(t).start())
    pass_on(f, 0).start()
    each(1, hf * W, lambda t: kv_copy(t).start())

    acc[...] = jnp.zeros_like(acc)
    dqacc[...] = jnp.zeros_like(dqacc)

    def relay(t):
        move = pass_on(f, t)
        move.wait_recv()
        move.start()

    lane1 = lax.broadcasted_iota(jnp.int32, (1, PAIR), 1)
    table = [pieces_of(HIDDEN)] + [pieces_of(math.log(n)) for n in range(1, n_slots + 2)]
    marks = []
    for p in range(F):
        seen = jnp.zeros((1, PAIR), F32)
        unseen = jnp.zeros((1, PAIR), F32)
        for gi in range(R):
            g = c + fs * gi
            own = jnp.where(p == g, 1, 0)
            count = own
            for slot in range(n_slots):
                count = count + jnp.where(part_ref[slot, g] == p, 1, 0)
            for e in range(SPLITS):
                here = lane1 == DH + SPLITS * gi + e
                for n in range(n_slots + 2):
                    if n < 2:
                        unseen = jnp.where(here & (own == n), table[n][e], unseen)
                    seen = jnp.where(here & (count == n), table[n][e], seen)
        marks.append((seen, unseen))

    lane = lax.broadcasted_iota(jnp.int32, (rows, PAIR), 1)
    row = lax.broadcasted_iota(jnp.int32, (rows, PAIR), 0)

    def prepare(u):
        aug, raw = [], []
        for d in range(per):
            ww = behind(u * per + d)
            for p in range(F):
                both = kv_in[p, ww].astype(F32)
                extra = jnp.where(row + ww * rows >= reg_ref[p], marks[p][0], marks[p][1])
                raw.append(both)
                aug.append(jnp.where(lane < DH, both, extra))
        raw = jnp.concatenate(raw, axis=0)
        keep = lax.broadcasted_iota(jnp.int32, (unit, PAIR), 1) >= DH
        kaug[u] = jnp.concatenate(aug, axis=0).astype(BF)
        vz[u] = jnp.where(keep, raw, 0.0).astype(BF)
        kt[u] = (raw * scale).T[:DH].astype(BF)

    def direct(u):
        each(max(u * per * hf, 1), (u + 1) * per * hf, relay)

    def settle(u):
        each(u * per * hf, (u + 1) * per * hf, lambda t: pass_on(sib, t).wait_recv())
        prepare(u)

    def rows_of(i):
        return pl.ds(pl.multiple_of(i * QC, QC), QC)

    def begin(b):
        top_ref[b] = jnp.full_like(top_ref[b], -3e38)
        total_ref[b] = jnp.zeros_like(total_ref[b])
        dsum_ref[b] = jnp.zeros_like(dsum_ref[b])

    def forth(u, i, b):
        at = rows_of(i)
        raw = rdot(kaug[u], qaug[at])
        old = top_ref[b]
        top = jnp.maximum(old, jnp.max(raw, axis=0, keepdims=True))
        keep = jnp.exp(old - top)
        expo = jnp.exp(raw - top)
        dprod = rdot(vz[u], xraw[at])
        sbuf[u, b] = expo
        dpbuf[u, b] = dprod
        tops[u, b] = top
        top_ref[b] = top
        total_ref[b] = total_ref[b] * keep + jnp.sum(expo, axis=0, keepdims=True)
        dsum_ref[b] = dsum_ref[b] * keep + jnp.sum(expo * dprod, axis=0, keepdims=True)

    def back(u, i, b):
        inv = 1.0 / total_ref[b]
        factor = jnp.exp(tops[u, b] - top_ref[b]) * inv
        prob = sbuf[u, b] * factor
        dscore = (prob * (dpbuf[u, b] - dsum_ref[b] * inv)).astype(BF)
        added = dot(jnp.concatenate([dscore, prob.astype(BF)], axis=1), qdz[i])
        acc[u] += added.reshape(per, F, rows, PAIR)
        dqacc[i] += dot(kt[u], dscore)

    def red_copy(u, dc):
        return pltpu.make_async_remote_copy(
            src_ref=red_send.at[u, dc - 1], dst_ref=red_in.at[u, dc - 1],
            send_sem=red_ss.at[u * (fs - 1) + dc - 1], recv_sem=red_rs.at[u * (fs - 1) + dc - 1],
            device_id=(a0 * fs + lax.rem(c + dc, fs), w), device_id_type=MESH)

    def ship_part(u):
        for dc in range(1, fs):
            for gi in range(R):
                red_send[u, dc - 1, gi] = acc[u, :, lax.rem(c + dc, fs) + fs * gi].astype(BF)
            red_copy(u, dc).start()

    def fin_copy(t):
        dw = lax.div(t, R)
        aa, ww = lax.rem(a0 + lax.rem(t, R), R), behind(dw)
        return pltpu.make_async_remote_copy(
            src_ref=fin_send.at[lax.div(dw, per), aa, lax.rem(dw, per)], dst_ref=fin_in.at[head],
            send_sem=fin_ss.at[t], recv_sem=fin_rs.at[head],
            device_id=(aa * fs + c, ww), device_id_type=MESH)

    def ship_home(u):
        for dc in range(1, fs):
            red_copy(u, dc).wait_recv()
        for gi in range(R):
            whole = acc[u, :, c + fs * gi]
            for dc in range(1, fs):
                whole = whole + red_in[u, dc - 1, gi].astype(F32)
            fin_send[u, gi] = whole.astype(BF)
        if u == 0:
            fin_in[head] = fin_send[0, a0, 0]
        each(max(u * per * R, 1), (u + 1) * per * R, lambda t: fin_copy(t).start())

    def take_queries():
        each(1, R * W, lambda t: qd_arrival(t).wait_recv())
        wide = lax.broadcasted_iota(jnp.int32, (nq, PAIR), 1)
        tall = lax.broadcasted_iota(jnp.int32, (nq, PAIR), 0)
        both = qd_in[...].astype(F32).reshape(nq, PAIR)
        mark = jnp.zeros((nq, PAIR), F32)
        for gi in range(R):
            mine = (tall >= gi * seq) & (tall < (gi + 1) * seq)
            mark = jnp.where(mine & (wide >= DH + SPLITS * gi) & (wide < DH + SPLITS * (gi + 1)), 1.0, mark)
        scaled = both * scale
        qaug[...] = jnp.where(wide < DH, scaled, mark).astype(BF)
        xraw[...] = both.astype(BF)
        qdz[:, :QC] = jnp.where(wide < DH, scaled, 0.0).astype(BF).reshape(n_chunks, QC, PAIR)
        qdz[:, QC:] = jnp.where(wide >= DH, both, 0.0).astype(BF).reshape(n_chunks, QC, PAIR)

    take_queries()
    if inline:
        each(0, n_chunks, begin)
        direct(0)
        for u in range(n_units):
            settle(u)
            forth(u, 0, 0)
            if u + 1 < n_units:
                direct(u + 1)
            each(1, n_chunks, lambda i: forth(u, i, i))
        for u in range(n_units):
            each(0, n_chunks, lambda i: back(u, i, i))
            ship_part(u)
            if u:
                ship_home(u - 1)
    else:
        for u in range(n_units):
            direct(u)
        for u in range(n_units):
            settle(u)

        def block(i):
            begin(0)
            each(0, n_units, lambda u: forth(u, i, 0))
            each(0, n_units, lambda u: back(u, i, 0))

        each(0, n_chunks, block)
        for u in range(n_units):
            ship_part(u)
        for u in range(n_units - 1):
            ship_home(u)

    def dq_copy(t):
        aa, ww = lax.rem(a0 + lax.rem(t, R), R), behind(lax.div(t, R))
        return pltpu.make_async_remote_copy(
            src_ref=dq_send.at[aa, ww], dst_ref=dq_in.at[head],
            send_sem=dq_ss.at[t], recv_sem=dq_rs.at[head],
            device_id=(aa * fs + c, ww), device_id_type=MESH)

    for i in range(n_chunks):
        dqs[i * QC:(i + 1) * QC] = jnp.concatenate([dqacc[i], jnp.zeros((DH, QC), F32)], axis=0).T
    for gi in range(R):
        for ww in range(W):
            base = gi * seq + ww * rows
            dq_send[gi, ww] = jnp.concatenate(
                [dqs[base:base + half, :DH], dqs[base + rows - half:base + rows, :DH]], axis=1).astype(BF)
    dq_in[head] = dq_send[a0, w]
    each(1, R * W, lambda t: dq_copy(t).start())
    ship_home(n_units - 1)

    each(1, R * W, lambda t: head_arrival(t, dq_in, dq_ss, dq_rs).wait_recv())
    for j in range(width // PAIR):
        cols = slice(j * PAIR, (j + 1) * PAIR)
        sides = []
        for h in (2 * j, 2 * j + 1):
            got = dq_in[h].astype(F32)
            sides.append(jnp.concatenate([got[:, :DH], got[2 * half - rows:, DH:]], axis=0))
        dq_out[0, :, cols] = jnp.concatenate(sides, axis=1).astype(BF)

    each(1, R * W, lambda t: head_arrival(t, fin_in, fin_ss, fin_rs).wait_recv())
    for j in range(width // PAIR):
        cols = slice(j * PAIR, (j + 1) * PAIR)
        one, two = fin_in[2 * j], fin_in[2 * j + 1]
        dk_out[0, :, cols] = jnp.concatenate([one[:, :DH], two[:, :DH]], axis=1)
        dv_out[0, :, cols] = jnp.concatenate([one[:, DH:], two[:, DH:]], axis=1)

    each(1, hf * W, lambda t: kv_copy(t).wait_send())
    each(0, hf * W, lambda t: pass_on(f, t).wait_send())
    each(1, R * W, lambda t: qd_copy(t).wait_send())
    each(1, R * W, lambda t: dq_copy(t).wait_send())
    each(1, R * W, lambda t: fin_copy(t).wait_send())
    for u in range(n_units):
        for dc in range(1, fs):
            red_copy(u, dc).wait_send()


def local(F, W, queries, keys_in, values_in, grad_out, partners, registers):
    _, rows, width = queries.shape
    heads = width // DH
    R = heads // W
    fs = F // R
    seq = rows * W
    nq = R * seq
    half = ((rows + 1) // 2 + 7) // 8 * 8
    inline = F * seq * nq * 8 <= 24 * 2 ** 20
    QC = next(b for b in ((384, 256, 128) if inline else (128,)) if nq % b == 0)
    held = nq // QC if inline else 1
    per = next(n for n in range(W, 0, -1) if W % n == 0 and (n == 1 or n * F * rows <= UNIT))
    units = W // per
    unit = per * F * rows
    vm = lambda *shape: pltpu.VMEM(shape, BF)
    vf = lambda *shape: pltpu.VMEM(shape, F32)
    dma = lambda n: pltpu.SemaphoreType.DMA((n,))
    out = jax.ShapeDtypeStruct((1, rows, width), BF)
    return pl.pallas_call(
        functools.partial(kernel, F, W, R, QC, inline),
        out_shape=(out, out, out),
        in_specs=[pl.BlockSpec(memory_space=pltpu.SMEM)] * 2 + [pl.BlockSpec(memory_space=pltpu.VMEM)] * 4,
        out_specs=(pl.BlockSpec(memory_space=pltpu.VMEM),) * 3,
        scratch_shapes=[
            vm(heads, rows, PAIR), vm(heads, rows, PAIR),
            vm(F, W, rows, PAIR), vm(R, W, rows, PAIR),
            vm(units, unit, PAIR), vm(units, unit, PAIR), vm(units, DH, unit),
            vm(nq, PAIR), vm(nq, PAIR), vm(nq // QC, 2 * QC, PAIR),
            vf(units, held, unit, QC), vf(units, held, unit, QC), vf(units, per, F, rows, PAIR),
            vf(nq // QC, DH, QC), vf(nq, PAIR),
            vf(units, held, 1, QC), vf(held, 1, QC), vf(held, 1, QC), vf(held, 1, QC),
            vm(units, fs - 1, R, per, rows, PAIR), vm(units, fs - 1, R, per, rows, PAIR),
            vm(units, R, per, rows, PAIR), vm(heads, rows, PAIR),
            vm(R, W, half, PAIR), vm(heads, half, PAIR),
            dma(F // 2 * W), dma(F // 2 * W), dma(F * W), dma(R * W), dma(R * W),
            dma(units * (fs - 1)), dma(units * (fs - 1)), dma(R * W), dma(heads), dma(R * W), dma(heads),
        ],
        compiler_params=pltpu.CompilerParams(
            collective_id=0, has_side_effects=True, vmem_limit_bytes=60 * 2 ** 20),
    )(partners.T, registers, queries, keys_in, values_in, grad_out)


def solution(mesh):
    spec = P("frame", "within", None)
    return jax.shard_map(
        functools.partial(local, mesh.shape["frame"], mesh.shape["within"]),
        mesh=mesh,
        in_specs=(spec, spec, spec, spec, P(), P()),
        out_specs=(spec, spec, spec),
        check_vma=False,
    )
```

```python
import functools
import math

import jax
import jax.numpy as jnp
import numpy as np
from jax import lax
from jax.experimental import pallas as pl
from jax.experimental.pallas import tpu as pltpu
from jax.sharding import PartitionSpec as P

DH = 64
PAIR = 2 * DH
SPLITS = 3
UNIT = 640
HIDDEN = -1e30
BF = jnp.bfloat16
F32 = jnp.float32
MESH = pl.DeviceIdType.MESH


def pieces_of(value):
    left, out = float(value), []
    for _ in range(SPLITS):
        part = float(np.asarray(left, dtype=jnp.bfloat16))
        out.append(part)
        left = left - part if abs(value) < 1e20 else 0.0
    return out


def rdot(a, b):
    return lax.dot_general(a, b, (((1,), (1,)), ((), ())), preferred_element_type=F32)


def dot(a, b):
    return jnp.dot(a, b, preferred_element_type=F32)


def each(lo, hi, do):
    def step(t, carry):
        do(t)
        return carry
    lax.fori_loop(lo, hi, step, 0)


def kernel(F, W, R, QC, inline, part_ref, reg_ref, q_ref, k_ref, v_ref, d_ref, dq_in, fin_in,
           kv_send, qd_send, kv_in, qd_in, kaug, vz, kt, qaug, xraw, qdz, sbuf, dpbuf, acc, dqacc, dqs,
           tops, top_ref, total_ref, dsum_ref,
           red_send, red_in, fin_send, dq_send, own_sem,
           kv_ss, fw_ss, kv_rs, qd_ss, qd_rs, red_ss, red_rs, fin_ss, fin_rs, dq_ss, dq_rs):
    fs = F // R
    hf = F // 2
    rows = q_ref.shape[1]
    width = q_ref.shape[2]
    seq = rows * W
    n_slots = part_ref.shape[0]
    scale = DH ** -0.5
    half = dq_send.shape[2]
    nq = R * seq
    n_chunks = nq // QC
    n_units, per = acc.shape[0], acc.shape[1]
    unit = per * F * rows
    f = lax.axis_index("frame")
    w = lax.axis_index("within")
    c = lax.rem(f, fs)
    a0 = lax.div(f, fs)
    sib = f + 1 - 2 * lax.rem(f, 2)
    head = w * R + a0

    barrier = pltpu.get_barrier_semaphore()

    def ahead(dw):
        return lax.rem(w + dw, W)

    def behind(dw):
        return lax.rem(w + W - dw, W)

    def greet(t):
        pl.semaphore_signal(barrier, inc=1, device_id=(lax.rem(f + 2 * lax.rem(t, hf), F), ahead(lax.div(t, hf))),
                            device_id_type=MESH)

    each(1, hf * W, greet)
    for dc in range(1, fs, 2):
        pl.semaphore_signal(barrier, inc=1, device_id=(a0 * fs + lax.rem(c + dc, fs), w), device_id_type=MESH)

    for first, second, out in ((q_ref, d_ref, qd_send), (k_ref, v_ref, kv_send)):
        for j in range(width // PAIR):
            cols = slice(j * PAIR, (j + 1) * PAIR)
            one = first[0, :, cols]
            two = second[0, :, cols]
            out[2 * j] = jnp.concatenate([one[:, :DH], two[:, :DH]], axis=1)
            out[2 * j + 1] = jnp.concatenate([one[:, DH:], two[:, DH:]], axis=1)
    kv_in[f, w] = kv_send[head]
    qd_in[a0, w] = qd_send[head]

    pl.semaphore_wait(barrier, hf * W - 1 + fs // 2)

    def kv_copy(t):
        ff = lax.rem(f + 2 * lax.rem(t, hf), F)
        ww = ahead(lax.div(t, hf))
        return pltpu.make_async_remote_copy(
            src_ref=kv_send.at[ww * R + lax.div(ff, fs)], dst_ref=kv_in.at[f, w],
            send_sem=kv_ss.at[t], recv_sem=kv_rs.at[f * W + w],
            device_id=(ff, ww), device_id_type=MESH)

    def pass_on(origin, t):
        ff = lax.rem(origin + F - 2 * lax.rem(t, hf), F)
        ww = behind(lax.div(t, hf))
        return pltpu.make_async_remote_copy(
            src_ref=kv_in.at[ff, ww], dst_ref=kv_in.at[ff, ww],
            send_sem=fw_ss.at[t], recv_sem=kv_rs.at[ff * W + ww],
            device_id=(sib, w), device_id_type=MESH)

    def qd_copy(t):
        aa, ww = lax.rem(a0 + lax.rem(t, R), R), ahead(lax.div(t, R))
        return pltpu.make_async_remote_copy(
            src_ref=qd_send.at[ww * R + aa], dst_ref=qd_in.at[a0, w],
            send_sem=qd_ss.at[t], recv_sem=qd_rs.at[a0 * W + w],
            device_id=(aa * fs + c, ww), device_id_type=MESH)

    def arrival(t, buffer, send, recv, index, source):
        return pltpu.make_async_remote_copy(
            src_ref=buffer.at[index], dst_ref=buffer.at[index], send_sem=send.at[t], recv_sem=recv,
            device_id=source, device_id_type=MESH)

    def qd_arrival(t):
        aa, ww = lax.rem(a0 + R - lax.rem(t, R), R), behind(lax.div(t, R))
        return arrival(t, qd_in, qd_ss, qd_rs.at[aa * W + ww], (aa, ww), (aa * fs + c, ww))

    def head_arrival(t, buffer, send, recv):
        aa, ww = lax.rem(a0 + R - lax.rem(t, R), R), ahead(lax.div(t, R))
        return arrival(t, buffer, send, recv.at[ww * R + aa], (ww * R + aa,), (aa * fs + c, ww))

    each(1, R * W, lambda t: qd_copy(t).start())
    pass_on(f, 0).start()
    each(1, hf * W, lambda t: kv_copy(t).start())

    acc[...] = jnp.zeros_like(acc)
    dqacc[...] = jnp.zeros_like(dqacc)

    def relay(t):
        move = pass_on(f, t)
        move.wait_recv()
        move.start()

    lane1 = lax.broadcasted_iota(jnp.int32, (1, PAIR), 1)
    table = [pieces_of(HIDDEN)] + [pieces_of(math.log(n)) for n in range(1, n_slots + 2)]
    marks = []
    for p in range(F):
        seen = jnp.zeros((1, PAIR), F32)
        unseen = jnp.zeros((1, PAIR), F32)
        for gi in range(R):
            g = c + fs * gi
            own = jnp.where(p == g, 1, 0)
            count = own
            for slot in range(n_slots):
                count = count + jnp.where(part_ref[slot, g] == p, 1, 0)
            for e in range(SPLITS):
                here = lane1 == DH + SPLITS * gi + e
                for n in range(n_slots + 2):
                    if n < 2:
                        unseen = jnp.where(here & (own == n), table[n][e], unseen)
                    seen = jnp.where(here & (count == n), table[n][e], seen)
        marks.append((seen, unseen))

    lane = lax.broadcasted_iota(jnp.int32, (rows, PAIR), 1)
    row = lax.broadcasted_iota(jnp.int32, (rows, PAIR), 0)

    def prepare(u):
        aug, raw = [], []
        for d in range(per):
            ww = behind(u * per + d)
            for p in range(F):
                both = kv_in[p, ww].astype(F32)
                extra = jnp.where(row + ww * rows >= reg_ref[p], marks[p][0], marks[p][1])
                raw.append(both)
                aug.append(jnp.where(lane < DH, both, extra))
        raw = jnp.concatenate(raw, axis=0)
        keep = lax.broadcasted_iota(jnp.int32, (unit, PAIR), 1) >= DH
        kaug[u] = jnp.concatenate(aug, axis=0).astype(BF)
        vz[u] = jnp.where(keep, raw, 0.0).astype(BF)
        kt[u] = (raw * scale).T[:DH].astype(BF)

    def direct(u):
        each(max(u * per * hf, 1), (u + 1) * per * hf, relay)

    def settle(u):
        each(u * per * hf, (u + 1) * per * hf, lambda t: pass_on(sib, t).wait_recv())
        prepare(u)

    def rows_of(i):
        return pl.ds(pl.multiple_of(i * QC, QC), QC)

    def begin(b):
        top_ref[b] = jnp.full_like(top_ref[b], -3e38)
        total_ref[b] = jnp.zeros_like(total_ref[b])
        dsum_ref[b] = jnp.zeros_like(dsum_ref[b])

    def forth(u, i, b):
        at = rows_of(i)
        raw = rdot(kaug[u], qaug[at])
        old = top_ref[b]
        top = jnp.maximum(old, jnp.max(raw, axis=0, keepdims=True))
        keep = jnp.exp(old - top)
        expo = jnp.exp(raw - top)
        dprod = rdot(vz[u], xraw[at])
        sbuf[u, b] = expo
        dpbuf[u, b] = dprod
        tops[u, b] = top
        top_ref[b] = top
        total_ref[b] = total_ref[b] * keep + jnp.sum(expo, axis=0, keepdims=True)
        dsum_ref[b] = dsum_ref[b] * keep + jnp.sum(expo * dprod, axis=0, keepdims=True)

    def back(u, i, b):
        inv = 1.0 / total_ref[b]
        factor = jnp.exp(tops[u, b] - top_ref[b]) * inv
        prob = sbuf[u, b] * factor
        dscore = (prob * (dpbuf[u, b] - dsum_ref[b] * inv)).astype(BF)
        added = dot(jnp.concatenate([dscore, prob.astype(BF)], axis=1), qdz[i])
        acc[u] += added.reshape(per, F, rows, PAIR)
        dqacc[i] += dot(kt[u], dscore)

    def own_copy(block, buffer, n):
        return pltpu.make_async_copy(block, buffer.at[head], own_sem.at[n])

    def red_copy(u, dc):
        return pltpu.make_async_remote_copy(
            src_ref=red_send.at[u, dc - 1], dst_ref=red_in.at[u, dc - 1],
            send_sem=red_ss.at[u * (fs - 1) + dc - 1], recv_sem=red_rs.at[u * (fs - 1) + dc - 1],
            device_id=(a0 * fs + lax.rem(c + dc, fs), w), device_id_type=MESH)

    def ship_part(u):
        for dc in range(1, fs):
            for gi in range(R):
                red_send[u, dc - 1, gi] = acc[u, :, lax.rem(c + dc, fs) + fs * gi].astype(BF)
            red_copy(u, dc).start()

    def fin_copy(t):
        dw = lax.div(t, R)
        aa, ww = lax.rem(a0 + lax.rem(t, R), R), behind(dw)
        return pltpu.make_async_remote_copy(
            src_ref=fin_send.at[lax.div(dw, per), aa, lax.rem(dw, per)], dst_ref=fin_in.at[head],
            send_sem=fin_ss.at[t], recv_sem=fin_rs.at[head],
            device_id=(aa * fs + c, ww), device_id_type=MESH)

    def ship_home(u):
        for dc in range(1, fs):
            red_copy(u, dc).wait_recv()
        for gi in range(R):
            whole = acc[u, :, c + fs * gi]
            for dc in range(1, fs):
                whole = whole + red_in[u, dc - 1, gi].astype(F32)
            fin_send[u, gi] = whole.astype(BF)
        if u == 0:
            own_copy(fin_send.at[0, a0, 0], fin_in, 0).start()
        each(max(u * per * R, 1), (u + 1) * per * R, lambda t: fin_copy(t).start())

    def take_queries():
        each(1, R * W, lambda t: qd_arrival(t).wait_recv())
        wide = lax.broadcasted_iota(jnp.int32, (nq, PAIR), 1)
        tall = lax.broadcasted_iota(jnp.int32, (nq, PAIR), 0)
        both = qd_in[...].astype(F32).reshape(nq, PAIR)
        mark = jnp.zeros((nq, PAIR), F32)
        for gi in range(R):
            mine = (tall >= gi * seq) & (tall < (gi + 1) * seq)
            mark = jnp.where(mine & (wide >= DH + SPLITS * gi) & (wide < DH + SPLITS * (gi + 1)), 1.0, mark)
        scaled = both * scale
        qaug[...] = jnp.where(wide < DH, scaled, mark).astype(BF)
        xraw[...] = both.astype(BF)
        qdz[:, :QC] = jnp.where(wide < DH, scaled, 0.0).astype(BF).reshape(n_chunks, QC, PAIR)
        qdz[:, QC:] = jnp.where(wide >= DH, both, 0.0).astype(BF).reshape(n_chunks, QC, PAIR)

    take_queries()
    if inline:
        each(0, n_chunks, begin)
        direct(0)
        for u in range(n_units):
            settle(u)
            forth(u, 0, 0)
            if u + 1 < n_units:
                direct(u + 1)
            each(1, n_chunks, lambda i: forth(u, i, i))
        for u in range(n_units):
            back(u, 0, 0)
            if u:
                ship_home(u - 1)
            each(1, n_chunks, lambda i: back(u, i, i))
            ship_part(u)
    else:
        for u in range(n_units):
            direct(u)
        for u in range(n_units):
            settle(u)

        def block(i):
            begin(0)
            each(0, n_units, lambda u: forth(u, i, 0))
            each(0, n_units, lambda u: back(u, i, 0))

        each(0, n_chunks, block)
        for u in range(n_units):
            ship_part(u)
        for u in range(n_units - 1):
            ship_home(u)

    def dq_copy(t):
        aa, ww = lax.rem(a0 + lax.rem(t, R), R), behind(lax.div(t, R))
        return pltpu.make_async_remote_copy(
            src_ref=dq_send.at[aa, ww], dst_ref=dq_in.at[head],
            send_sem=dq_ss.at[t], recv_sem=dq_rs.at[head],
            device_id=(aa * fs + c, ww), device_id_type=MESH)

    for i in range(n_chunks):
        dqs[i * QC:(i + 1) * QC] = jnp.concatenate([dqacc[i], jnp.zeros((DH, QC), F32)], axis=0).T
    for gi in range(R):
        for ww in range(W):
            base = gi * seq + ww * rows
            dq_send[gi, ww] = jnp.concatenate(
                [dqs[base:base + half, :DH], dqs[base + rows - half:base + rows, :DH]], axis=1).astype(BF)
    own_copy(dq_send.at[a0, w], dq_in, 1).start()
    each(1, R * W, lambda t: dq_copy(t).start())
    ship_home(n_units - 1)

    each(1, R * W, lambda t: head_arrival(t, dq_in, dq_ss, dq_rs).wait_recv())
    each(1, R * W, lambda t: head_arrival(t, fin_in, fin_ss, fin_rs).wait_recv())
    each(1, hf * W, lambda t: kv_copy(t).wait_send())
    each(0, hf * W, lambda t: pass_on(f, t).wait_send())
    each(1, R * W, lambda t: qd_copy(t).wait_send())
    own_copy(fin_send.at[0, a0, 0], fin_in, 0).wait()
    own_copy(dq_send.at[a0, w], dq_in, 1).wait()
    each(1, R * W, lambda t: dq_copy(t).wait_send())
    each(1, R * W, lambda t: fin_copy(t).wait_send())
    for u in range(n_units):
        for dc in range(1, fs):
            red_copy(u, dc).wait_send()


def tokens_again(dq_in, fin_in, dq_out, dk_out, dv_out):
    half, rows, width = dq_in.shape[1], dq_out.shape[1], dq_out.shape[2]
    for j in range(width // PAIR):
        cols = slice(j * PAIR, (j + 1) * PAIR)
        sides = []
        for h in (2 * j, 2 * j + 1):
            got = dq_in[h].astype(F32)
            sides.append(jnp.concatenate([got[:, :DH], got[2 * half - rows:, DH:]], axis=0))
        dq_out[0, :, cols] = jnp.concatenate(sides, axis=1).astype(BF)

    for j in range(width // PAIR):
        cols = slice(j * PAIR, (j + 1) * PAIR)
        one, two = fin_in[2 * j], fin_in[2 * j + 1]
        dk_out[0, :, cols] = jnp.concatenate([one[:, :DH], two[:, :DH]], axis=1)
        dv_out[0, :, cols] = jnp.concatenate([one[:, DH:], two[:, DH:]], axis=1)


def local(F, W, queries, keys_in, values_in, grad_out, partners, registers):
    _, rows, width = queries.shape
    heads = width // DH
    R = heads // W
    fs = F // R
    seq = rows * W
    nq = R * seq
    half = ((rows + 1) // 2 + 7) // 8 * 8
    inline = F * seq * nq * 8 <= 24 * 2 ** 20
    QC = next(b for b in ((576, 384, 128) if inline else (128,)) if nq % b == 0)
    held = nq // QC if inline else 1
    per = next(n for n in range(W, 0, -1) if W % n == 0 and (n == 1 or n * F * rows <= UNIT))
    units = W // per
    unit = per * F * rows
    vm = lambda *shape: pltpu.VMEM(shape, BF)
    vf = lambda *shape: pltpu.VMEM(shape, F32)
    dma = lambda n: pltpu.SemaphoreType.DMA((n,))
    out = jax.ShapeDtypeStruct((1, rows, width), BF)
    dq_heads, kv_heads = pl.pallas_call(
        functools.partial(kernel, F, W, R, QC, inline),
        out_shape=(jax.ShapeDtypeStruct((heads, half, PAIR), BF), jax.ShapeDtypeStruct((heads, rows, PAIR), BF)),
        in_specs=[pl.BlockSpec(memory_space=pltpu.SMEM)] * 2 + [pl.BlockSpec(memory_space=pltpu.VMEM)] * 4,
        out_specs=(pl.BlockSpec(memory_space=pl.ANY),) * 2,
        scratch_shapes=[
            vm(heads, rows, PAIR), vm(heads, rows, PAIR),
            vm(F, W, rows, PAIR), vm(R, W, rows, PAIR),
            vm(units, unit, PAIR), vm(units, unit, PAIR), vm(units, DH, unit),
            vm(nq, PAIR), vm(nq, PAIR), vm(nq // QC, 2 * QC, PAIR),
            vf(units, held, unit, QC), vf(units, held, unit, QC), vf(units, per, F, rows, PAIR),
            vf(nq // QC, DH, QC), vf(nq, PAIR),
            vf(units, held, 1, QC), vf(held, 1, QC), vf(held, 1, QC), vf(held, 1, QC),
            vm(units, fs - 1, R, per, rows, PAIR), vm(units, fs - 1, R, per, rows, PAIR),
            vm(units, R, per, rows, PAIR), vm(R, W, half, PAIR), dma(2),
            dma(F // 2 * W), dma(F // 2 * W), dma(F * W), dma(R * W), dma(R * W),
            dma(units * (fs - 1)), dma(units * (fs - 1)), dma(R * W), dma(heads), dma(R * W), dma(heads),
        ],
        compiler_params=pltpu.CompilerParams(
            collective_id=0, has_side_effects=True, vmem_limit_bytes=60 * 2 ** 20),
    )(partners.T, registers, queries, keys_in, values_in, grad_out)
    return pl.pallas_call(
        tokens_again,
        out_shape=(out, out, out),
        in_specs=[pl.BlockSpec(memory_space=pltpu.VMEM)] * 2,
        out_specs=(pl.BlockSpec(memory_space=pltpu.VMEM),) * 3,
    )(dq_heads, kv_heads)


def solution(mesh):
    spec = P("frame", "within", None)
    return jax.shard_map(
        functools.partial(local, mesh.shape["frame"], mesh.shape["within"]),
        mesh=mesh,
        in_specs=(spec, spec, spec, spec, P(), P()),
        out_specs=(spec, spec, spec),
        check_vma=False,
    )
```

```python
import functools
import math

import jax
import jax.numpy as jnp
import numpy as np
from jax import lax
from jax.experimental import pallas as pl
from jax.experimental.pallas import tpu as pltpu
from jax.sharding import PartitionSpec as P

DH = 64
PAIR = 2 * DH
SPLITS = 3
UNIT = 640
HIDDEN = -1e30
BF = jnp.bfloat16
F32 = jnp.float32
MESH = pl.DeviceIdType.MESH


def pieces_of(value):
    left, out = float(value), []
    for _ in range(SPLITS):
        part = float(np.asarray(left, dtype=jnp.bfloat16))
        out.append(part)
        left = left - part if abs(value) < 1e20 else 0.0
    return out


def rdot(a, b):
    return lax.dot_general(a, b, (((1,), (1,)), ((), ())), preferred_element_type=F32)


def dot(a, b):
    return jnp.dot(a, b, preferred_element_type=F32)


def each(lo, hi, do):
    def step(t, carry):
        do(t)
        return carry
    lax.fori_loop(lo, hi, step, 0)


def kernel(F, W, R, QC, inline, part_ref, reg_ref, q_ref, k_ref, v_ref, d_ref, dq_in, fin_in,
           kv_send, qd_send, kv_in, qd_in, kaug, vz, kt, qaug, xraw, qdz, sbuf, dpbuf, acc, dqacc, dqs,
           tops, top_ref, total_ref, dsum_ref,
           red_send, red_in, fin_send, dq_send, own_sem,
           kv_ss, fw_ss, kv_rs, qd_ss, qd_rs, red_ss, red_rs, fin_ss, fin_rs, dq_ss, dq_rs):
    fs = F // R
    hf = F // 2
    rows = q_ref.shape[1]
    width = q_ref.shape[2]
    seq = rows * W
    n_slots = part_ref.shape[0]
    scale = DH ** -0.5
    half = dq_send.shape[2]
    nq = R * seq
    n_chunks = nq // QC
    n_units, per = acc.shape[0], acc.shape[1]
    unit = per * F * rows
    f = lax.axis_index("frame")
    w = lax.axis_index("within")
    c = lax.rem(f, fs)
    a0 = lax.div(f, fs)
    sib = f + 1 - 2 * lax.rem(f, 2)
    head = w * R + a0

    barrier = pltpu.get_barrier_semaphore()

    def ahead(dw):
        return lax.rem(w + W - dw, W)

    def behind(dw):
        return lax.rem(w + dw, W)

    def greet(t):
        pl.semaphore_signal(barrier, inc=1, device_id=(lax.rem(f + 2 * lax.rem(t, hf), F), ahead(lax.div(t, hf))),
                            device_id_type=MESH)

    each(1, hf * W, greet)
    for dc in range(1, fs, 2):
        pl.semaphore_signal(barrier, inc=1, device_id=(a0 * fs + lax.rem(c + dc, fs), w), device_id_type=MESH)

    for first, second, out in ((q_ref, d_ref, qd_send), (k_ref, v_ref, kv_send)):
        for j in range(width // PAIR):
            cols = slice(j * PAIR, (j + 1) * PAIR)
            one = first[0, :, cols]
            two = second[0, :, cols]
            out[2 * j] = jnp.concatenate([one[:, :DH], two[:, :DH]], axis=1)
            out[2 * j + 1] = jnp.concatenate([one[:, DH:], two[:, DH:]], axis=1)
    kv_in[f, w] = kv_send[head]
    qd_in[a0, w] = qd_send[head]

    pl.semaphore_wait(barrier, hf * W - 1 + fs // 2)

    def kv_copy(t):
        ff = lax.rem(f + 2 * lax.rem(t, hf), F)
        ww = ahead(lax.div(t, hf))
        return pltpu.make_async_remote_copy(
            src_ref=kv_send.at[ww * R + lax.div(ff, fs)], dst_ref=kv_in.at[f, w],
            send_sem=kv_ss.at[t], recv_sem=kv_rs.at[f * W + w],
            device_id=(ff, ww), device_id_type=MESH)

    def pass_on(origin, t):
        ff = lax.rem(origin + F - 2 * lax.rem(t, hf), F)
        ww = behind(lax.div(t, hf))
        return pltpu.make_async_remote_copy(
            src_ref=kv_in.at[ff, ww], dst_ref=kv_in.at[ff, ww],
            send_sem=fw_ss.at[t], recv_sem=kv_rs.at[ff * W + ww],
            device_id=(sib, w), device_id_type=MESH)

    def qd_copy(t):
        aa, ww = lax.rem(a0 + lax.rem(t, R), R), ahead(lax.div(t, R))
        return pltpu.make_async_remote_copy(
            src_ref=qd_send.at[ww * R + aa], dst_ref=qd_in.at[a0, w],
            send_sem=qd_ss.at[t], recv_sem=qd_rs.at[a0 * W + w],
            device_id=(aa * fs + c, ww), device_id_type=MESH)

    def arrival(t, buffer, send, recv, index, source):
        return pltpu.make_async_remote_copy(
            src_ref=buffer.at[index], dst_ref=buffer.at[index], send_sem=send.at[t], recv_sem=recv,
            device_id=source, device_id_type=MESH)

    def qd_arrival(t):
        aa, ww = lax.rem(a0 + R - lax.rem(t, R), R), behind(lax.div(t, R))
        return arrival(t, qd_in, qd_ss, qd_rs.at[aa * W + ww], (aa, ww), (aa * fs + c, ww))

    def head_arrival(t, buffer, send, recv):
        aa, ww = lax.rem(a0 + R - lax.rem(t, R), R), ahead(lax.div(t, R))
        return arrival(t, buffer, send, recv.at[ww * R + aa], (ww * R + aa,), (aa * fs + c, ww))

    each(1, R * W, lambda t: qd_copy(t).start())
    pass_on(f, 0).start()
    each(1, hf * W, lambda t: kv_copy(t).start())

    acc[...] = jnp.zeros_like(acc)
    dqacc[...] = jnp.zeros_like(dqacc)

    def relay(t):
        move = pass_on(f, t)
        move.wait_recv()
        move.start()

    lane1 = lax.broadcasted_iota(jnp.int32, (1, PAIR), 1)
    table = [pieces_of(HIDDEN)] + [pieces_of(math.log(n)) for n in range(1, n_slots + 2)]
    marks = []
    for p in range(F):
        seen = jnp.zeros((1, PAIR), F32)
        unseen = jnp.zeros((1, PAIR), F32)
        for gi in range(R):
            g = c + fs * gi
            own = jnp.where(p == g, 1, 0)
            count = own
            for slot in range(n_slots):
                count = count + jnp.where(part_ref[slot, g] == p, 1, 0)
            for e in range(SPLITS):
                here = lane1 == DH + SPLITS * gi + e
                for n in range(n_slots + 2):
                    if n < 2:
                        unseen = jnp.where(here & (own == n), table[n][e], unseen)
                    seen = jnp.where(here & (count == n), table[n][e], seen)
        marks.append((seen, unseen))

    lane = lax.broadcasted_iota(jnp.int32, (rows, PAIR), 1)
    row = lax.broadcasted_iota(jnp.int32, (rows, PAIR), 0)

    def prepare(u):
        aug, raw = [], []
        for d in range(per):
            ww = behind(u * per + d)
            for p in range(F):
                both = kv_in[p, ww].astype(F32)
                extra = jnp.where(row + ww * rows >= reg_ref[p], marks[p][0], marks[p][1])
                raw.append(both)
                aug.append(jnp.where(lane < DH, both, extra))
        raw = jnp.concatenate(raw, axis=0)
        keep = lax.broadcasted_iota(jnp.int32, (unit, PAIR), 1) >= DH
        kaug[u] = jnp.concatenate(aug, axis=0).astype(BF)
        vz[u] = jnp.where(keep, raw, 0.0).astype(BF)
        kt[u] = (raw * scale).T[:DH].astype(BF)

    def direct(u):
        each(max(u * per * hf, 1), (u + 1) * per * hf, relay)

    def settle(u):
        each(u * per * hf, (u + 1) * per * hf, lambda t: pass_on(sib, t).wait_recv())
        prepare(u)

    def rows_of(i):
        return pl.ds(pl.multiple_of(i * QC, QC), QC)

    def begin(b):
        top_ref[b] = jnp.full_like(top_ref[b], -3e38)
        total_ref[b] = jnp.zeros_like(total_ref[b])
        dsum_ref[b] = jnp.zeros_like(dsum_ref[b])

    def forth(u, i, b):
        at = rows_of(i)
        raw = rdot(kaug[u], qaug[at])
        old = top_ref[b]
        top = jnp.maximum(old, jnp.max(raw, axis=0, keepdims=True))
        keep = jnp.exp(old - top)
        expo = jnp.exp(raw - top)
        dprod = rdot(vz[u], xraw[at])
        sbuf[u, b] = expo
        dpbuf[u, b] = dprod
        tops[u, b] = top
        top_ref[b] = top
        total_ref[b] = total_ref[b] * keep + jnp.sum(expo, axis=0, keepdims=True)
        dsum_ref[b] = dsum_ref[b] * keep + jnp.sum(expo * dprod, axis=0, keepdims=True)

    def back(u, i, b):
        inv = 1.0 / total_ref[b]
        factor = jnp.exp(tops[u, b] - top_ref[b]) * inv
        prob = sbuf[u, b] * factor
        dscore = (prob * (dpbuf[u, b] - dsum_ref[b] * inv)).astype(BF)
        added = dot(jnp.concatenate([dscore, prob.astype(BF)], axis=1), qdz[i])
        acc[u] += added.reshape(per, F, rows, PAIR)
        dqacc[i] += dot(kt[u], dscore)

    def own_copy(block, buffer, n):
        return pltpu.make_async_copy(block, buffer.at[head], own_sem.at[n])

    def red_copy(u, dc):
        return pltpu.make_async_remote_copy(
            src_ref=red_send.at[u, dc - 1], dst_ref=red_in.at[u, dc - 1],
            send_sem=red_ss.at[u * (fs - 1) + dc - 1], recv_sem=red_rs.at[u * (fs - 1) + dc - 1],
            device_id=(a0 * fs + lax.rem(c + dc, fs), w), device_id_type=MESH)

    def ship_part(u):
        for dc in range(1, fs):
            for gi in range(R):
                red_send[u, dc - 1, gi] = acc[u, :, lax.rem(c + dc, fs) + fs * gi].astype(BF)
            red_copy(u, dc).start()

    def fin_copy(t):
        dw = lax.div(t, R)
        aa, ww = lax.rem(a0 + lax.rem(t, R), R), behind(dw)
        return pltpu.make_async_remote_copy(
            src_ref=fin_send.at[lax.div(dw, per), aa, lax.rem(dw, per)], dst_ref=fin_in.at[head],
            send_sem=fin_ss.at[t], recv_sem=fin_rs.at[head],
            device_id=(aa * fs + c, ww), device_id_type=MESH)

    def ship_home(u):
        for dc in range(1, fs):
            red_copy(u, dc).wait_recv()
        for gi in range(R):
            whole = acc[u, :, c + fs * gi]
            for dc in range(1, fs):
                whole = whole + red_in[u, dc - 1, gi].astype(F32)
            fin_send[u, gi] = whole.astype(BF)
        if u == 0:
            own_copy(fin_send.at[0, a0, 0], fin_in, 0).start()
        each(max(u * per * R, 1), (u + 1) * per * R, lambda t: fin_copy(t).start())

    def take_queries():
        each(1, R * W, lambda t: qd_arrival(t).wait_recv())
        wide = lax.broadcasted_iota(jnp.int32, (nq, PAIR), 1)
        tall = lax.broadcasted_iota(jnp.int32, (nq, PAIR), 0)
        both = qd_in[...].astype(F32).reshape(nq, PAIR)
        mark = jnp.zeros((nq, PAIR), F32)
        for gi in range(R):
            mine = (tall >= gi * seq) & (tall < (gi + 1) * seq)
            mark = jnp.where(mine & (wide >= DH + SPLITS * gi) & (wide < DH + SPLITS * (gi + 1)), 1.0, mark)
        scaled = both * scale
        qaug[...] = jnp.where(wide < DH, scaled, mark).astype(BF)
        xraw[...] = both.astype(BF)
        qdz[:, :QC] = jnp.where(wide < DH, scaled, 0.0).astype(BF).reshape(n_chunks, QC, PAIR)
        qdz[:, QC:] = jnp.where(wide >= DH, both, 0.0).astype(BF).reshape(n_chunks, QC, PAIR)

    take_queries()
    if inline:
        each(0, n_chunks, begin)
        direct(0)
        for u in range(n_units):
            settle(u)
            forth(u, 0, 0)
            if u + 1 < n_units:
                direct(u + 1)
            each(1, n_chunks, lambda i: forth(u, i, i))
        for u in range(n_units):
            back(u, 0, 0)
            if u:
                ship_home(u - 1)
            each(1, n_chunks, lambda i: back(u, i, i))
            ship_part(u)
    else:
        for u in range(n_units):
            direct(u)
        for u in range(n_units):
            settle(u)

        def block(i):
            begin(0)
            each(0, n_units, lambda u: forth(u, i, 0))
            each(0, n_units, lambda u: back(u, i, 0))

        each(0, n_chunks, block)
        for u in range(n_units):
            ship_part(u)
        for u in range(n_units - 1):
            ship_home(u)

    def dq_copy(t):
        aa, ww = lax.rem(a0 + lax.rem(t, R), R), behind(lax.div(t, R))
        return pltpu.make_async_remote_copy(
            src_ref=dq_send.at[aa, ww], dst_ref=dq_in.at[head],
            send_sem=dq_ss.at[t], recv_sem=dq_rs.at[head],
            device_id=(aa * fs + c, ww), device_id_type=MESH)

    for i in range(n_chunks):
        dqs[i * QC:(i + 1) * QC] = jnp.concatenate([dqacc[i], jnp.zeros((DH, QC), F32)], axis=0).T
    for gi in range(R):
        for ww in range(W):
            base = gi * seq + ww * rows
            dq_send[gi, ww] = jnp.concatenate(
                [dqs[base:base + half, :DH], dqs[base + rows - half:base + rows, :DH]], axis=1).astype(BF)
    own_copy(dq_send.at[a0, w], dq_in, 1).start()
    each(1, R * W, lambda t: dq_copy(t).start())
    ship_home(n_units - 1)

    each(1, R * W, lambda t: head_arrival(t, dq_in, dq_ss, dq_rs).wait_recv())
    each(1, R * W, lambda t: head_arrival(t, fin_in, fin_ss, fin_rs).wait_recv())
    each(1, hf * W, lambda t: kv_copy(t).wait_send())
    each(0, hf * W, lambda t: pass_on(f, t).wait_send())
    each(1, R * W, lambda t: qd_copy(t).wait_send())
    own_copy(fin_send.at[0, a0, 0], fin_in, 0).wait()
    own_copy(dq_send.at[a0, w], dq_in, 1).wait()
    each(1, R * W, lambda t: dq_copy(t).wait_send())
    each(1, R * W, lambda t: fin_copy(t).wait_send())
    for u in range(n_units):
        for dc in range(1, fs):
            red_copy(u, dc).wait_send()


def tokens_again(dq_in, fin_in, dq_out, dk_out, dv_out):
    half, rows, width = dq_in.shape[1], dq_out.shape[1], dq_out.shape[2]
    for j in range(width // PAIR):
        cols = slice(j * PAIR, (j + 1) * PAIR)
        sides = []
        for h in (2 * j, 2 * j + 1):
            got = dq_in[h].astype(F32)
            sides.append(jnp.concatenate([got[:, :DH], got[2 * half - rows:, DH:]], axis=0))
        dq_out[0, :, cols] = jnp.concatenate(sides, axis=1).astype(BF)

    for j in range(width // PAIR):
        cols = slice(j * PAIR, (j + 1) * PAIR)
        one, two = fin_in[2 * j], fin_in[2 * j + 1]
        dk_out[0, :, cols] = jnp.concatenate([one[:, :DH], two[:, :DH]], axis=1)
        dv_out[0, :, cols] = jnp.concatenate([one[:, DH:], two[:, DH:]], axis=1)


def local(F, W, queries, keys_in, values_in, grad_out, partners, registers):
    _, rows, width = queries.shape
    heads = width // DH
    R = heads // W
    fs = F // R
    seq = rows * W
    nq = R * seq
    half = ((rows + 1) // 2 + 7) // 8 * 8
    inline = F * seq * nq * 8 <= 24 * 2 ** 20
    QC = next(b for b in ((576, 384, 128) if inline else (128,)) if nq % b == 0)
    held = nq // QC if inline else 1
    per = next(n for n in range(W, 0, -1) if W % n == 0 and (n == 1 or n * F * rows <= UNIT))
    units = W // per
    unit = per * F * rows
    vm = lambda *shape: pltpu.VMEM(shape, BF)
    vf = lambda *shape: pltpu.VMEM(shape, F32)
    dma = lambda n: pltpu.SemaphoreType.DMA((n,))
    out = jax.ShapeDtypeStruct((1, rows, width), BF)
    dq_heads, kv_heads = pl.pallas_call(
        functools.partial(kernel, F, W, R, QC, inline),
        out_shape=(jax.ShapeDtypeStruct((heads, half, PAIR), BF), jax.ShapeDtypeStruct((heads, rows, PAIR), BF)),
        in_specs=[pl.BlockSpec(memory_space=pltpu.SMEM)] * 2 + [pl.BlockSpec(memory_space=pltpu.VMEM)] * 4,
        out_specs=(pl.BlockSpec(memory_space=pl.ANY),) * 2,
        scratch_shapes=[
            vm(heads, rows, PAIR), vm(heads, rows, PAIR),
            vm(F, W, rows, PAIR), vm(R, W, rows, PAIR),
            vm(units, unit, PAIR), vm(units, unit, PAIR), vm(units, DH, unit),
            vm(nq, PAIR), vm(nq, PAIR), vm(nq // QC, 2 * QC, PAIR),
            vf(units, held, unit, QC), vf(units, held, unit, QC), vf(units, per, F, rows, PAIR),
            vf(nq // QC, DH, QC), vf(nq, PAIR),
            vf(units, held, 1, QC), vf(held, 1, QC), vf(held, 1, QC), vf(held, 1, QC),
            vm(units, fs - 1, R, per, rows, PAIR), vm(units, fs - 1, R, per, rows, PAIR),
            vm(units, R, per, rows, PAIR), vm(R, W, half, PAIR), dma(2),
            dma(F // 2 * W), dma(F // 2 * W), dma(F * W), dma(R * W), dma(R * W),
            dma(units * (fs - 1)), dma(units * (fs - 1)), dma(R * W), dma(heads), dma(R * W), dma(heads),
        ],
        compiler_params=pltpu.CompilerParams(
            collective_id=0, has_side_effects=True, vmem_limit_bytes=60 * 2 ** 20),
    )(partners.T, registers, queries, keys_in, values_in, grad_out)
    return pl.pallas_call(
        tokens_again,
        out_shape=(out, out, out),
        in_specs=[pl.BlockSpec(memory_space=pltpu.VMEM)] * 2,
        out_specs=(pl.BlockSpec(memory_space=pltpu.VMEM),) * 3,
    )(dq_heads, kv_heads)


def solution(mesh):
    spec = P("frame", "within", None)
    return jax.shard_map(
        functools.partial(local, mesh.shape["frame"], mesh.shape["within"]),
        mesh=mesh,
        in_specs=(spec, spec, spec, spec, P(), P()),
        out_specs=(spec, spec, spec),
        check_vma=False,
    )
```
